32 devices in a mesh: seq: 8 (over z, y), tp: 4 (over x, core).
Axes of the slice: x: 2, y: 2, z: 4, core: 2. Of those that a mesh axis runs over, the one named last changes fastest.
Arguments:
- attention_output: bfloat16 [6144, 4096], P('seq', 'tp'), may hold values from -6 to 6
- output_gradient: bfloat16 [6144, 4096], P('seq', 'tp'), may hold values from -6 to 6
- output_weight: bfloat16 [4096, 4096], P('tp'), may hold values from -0.09375 to 0.09375
- adapter_down: bfloat16 [32, 64, 4096], P('seq', None, 'tp'), may hold values from -0.09375 to 0.09375
- adapter_up: bfloat16 [32, 64, 4096], P('seq', None, 'tp'), may hold values from -0.75 to 0.75
- momentum_down: float32 [32, 64, 4096], P('seq', None, 'tp'), may hold values from -6 to 6
- momentum_up: float32 [32, 64, 4096], P('seq', None, 'tp'), may hold values from -6 to 6
- tenant_storage_row: int32 [32], replicated, may hold values from 0 to 31, as said below
- slot_tenant_index: int32 [8, 4], replicated, may hold values from 0 to 31, as said below
- slot_token_rows: int32 [8, 4], replicated, may hold values from 1 to 288, 768 in all within a row
Outputs:
- out_act: bfloat16 [6144, 4096], P('seq', 'tp')
- in_grad: bfloat16 [6144, 4096], P('seq', 'tp')
- step_down: float32 [32, 64, 4096], P('seq', None, 'tp')
- step_up: float32 [32, 64, 4096], P('seq', None, 'tp')
- new_moment_down: float32 [32, 64, 4096], P('seq', None, 'tp')
- new_moment_up: float32 [32, 64, 4096], P('seq', None, 'tp')
The draws below stay inside these ranges and needn't reach their ends.
Inputs may be any that keep to these rules, and one draw needn't show every extreme that they name: A permutation: tenant t's adapters and momenta are row tenant_storage_row[t], owned by seq index tenant_storage_row[t] // 4. `slot_tenant_index`: the 4 tenants of one seq index have distinct owners; a tenant may stand on several seq indices or on none. `slot_token_rows`: each row sums to 768.
All inputs are finite; a program needn't handle non-finite values.
Results may differ from the reference program's by a relative error of at most 0.014.
Values may be sent and summed in bfloat16 or wider, within the bound.
A program may use at most 128 MiB of HBM per device.

```python
import math
import jax
import jax.numpy as jnp
import numpy as np
from jax import lax

FEATURES_INPUT = 4096
FEATURES_OUTPUT = 4096
ADAPTER_RANK = 64
TOKEN_ROWS_LOCAL = 768
SLOTS_PER_SEQ = 4
TEN_DEV = 4
TENANT_TOTAL = 32
TOKENS = 6144
MOST = 288
N_SEQ = 8
N_TP = 4


def layout_tables(key):
    folded = jax.random.fold_in(key, 11)
    keys = jax.random.split(folded, 3)
    storage = jax.random.permutation(keys[0], TENANT_TOTAL).astype(jnp.int32)
    inverse = jnp.zeros((TENANT_TOTAL,), jnp.int32).at[storage].set(jnp.arange(TENANT_TOTAL, dtype=jnp.int32))
    row_keys = jax.random.split(keys[1], N_SEQ)
    owners = jax.vmap(lambda single: jax.random.permutation(single, N_SEQ))(row_keys)[:, :SLOTS_PER_SEQ].astype(jnp.int32)
    within = jax.random.randint(keys[2], (N_SEQ, SLOTS_PER_SEQ), 0, TEN_DEV).astype(jnp.int32)
    tenants = inverse[owners * TEN_DEV + within]
    return (storage, tenants.astype(jnp.int32))


def draw_tenant_storage_row(key, part):
    return layout_tables(key)[0]


def draw_slot_tenant_index(key, part):
    return layout_tables(key)[1]


def steps_of(own_key, dims, cuts, low, top_value):
    def one(axis_at, shards_of):
        steps = jax.random.uniform(jax.random.fold_in(jax.random.fold_in(own_key, 6), axis_at), (shards_of,), jnp.float32, low / len(cuts), top_value / len(cuts))
        return jnp.repeat(jnp.exp(steps), dims[axis_at] // shards_of).reshape((-1,) + (1,) * (len(dims) - axis_at - 1))

    loudness = one(*cuts[0])
    for cut in cuts[1:]:
        loudness = loudness * one(*cut)
    return loudness


def profile(amount, total, most, lean):
    loads = [(1 << 20) // math.isqrt(standing ** lean) + 1 for standing in range(2, amount + 1)]
    surplus, holding = total - most - (amount - 1), [1] * (amount - 1)
    while surplus > 0:
        candidates = [i for i in range(amount - 1) if holding[i] < most]
        mass, left = sum([loads[i] for i in candidates]), surplus
        for i in candidates:
            extra = min(most - holding[i], max(1, left * loads[i] // mass), surplus)
            holding[i] = holding[i] + extra
            surplus = surplus - extra
    return np.array([most] + holding)


def uneven(rng, number_of, total, bound, skew):
    if number_of == 2:
        one = jax.random.randint(rng, (), max(1, total - bound), min(bound, total - 1) + 1)
        return jnp.stack([one, total - one])
    lengths = jnp.asarray(profile(number_of, total, bound, skew), jnp.int32)
    twos = (number_of - 1) // 2
    donor, receiver = lengths[1:1 + 2 * twos:2], lengths[2:2 + 2 * twos:2]
    slack = jnp.minimum(donor - 1, bound - receiver)
    moved = jax.random.randint(jax.random.fold_in(rng, 1), (twos,), 0, 1 << 20) % (slack + 1)
    lengths = lengths.at[1:1 + 2 * twos:2].set(donor - moved).at[2:2 + 2 * twos:2].set(receiver + moved)
    return lengths[jax.random.permutation(jax.random.fold_in(rng, 2), number_of)]


def centred(stream_key, dims, scale, bound, cuts=(), held_as=jnp.bfloat16):
    result = jax.random.normal(stream_key, dims, jnp.float32) * scale
    if len(cuts) > 0:
        result = steps_of(stream_key, dims, cuts, -0.22, 0.18) * result
    return jnp.clip(result, min=-bound, max=bound).astype(held_as)


def setup_inputs(seed: int = 0) -> dict:
    arg_keys = jax.random.split(jax.random.key(seed), 11)
    attention_output = centred(arg_keys[0], (TOKENS, FEATURES_INPUT), 1.0, 6.0, ((0, 8), (1, 4)))
    output_gradient = centred(arg_keys[1], (TOKENS, FEATURES_OUTPUT), 1.0, 6.0, ((0, 8), (1, 4)))
    output_weight = centred(arg_keys[2], (FEATURES_INPUT, FEATURES_OUTPUT), FEATURES_INPUT ** -0.5, 0.09375, ((0, 4),))
    adapter_down = centred(arg_keys[3], (TENANT_TOTAL, ADAPTER_RANK, FEATURES_INPUT), FEATURES_INPUT ** -0.5, 0.09375, ((0, 8), (2, 4)))
    adapter_up = centred(arg_keys[4], (TENANT_TOTAL, ADAPTER_RANK, FEATURES_OUTPUT), ADAPTER_RANK ** -0.5, 0.75, ((0, 8), (2, 4)))
    momentum_down = centred(arg_keys[5], (TENANT_TOTAL, ADAPTER_RANK, FEATURES_INPUT), 1.0, 6.0, ((0, 8), (2, 4)), jnp.float32)
    momentum_up = centred(arg_keys[6], (TENANT_TOTAL, ADAPTER_RANK, FEATURES_OUTPUT), 1.0, 6.0, ((0, 8), (2, 4)), jnp.float32)
    tenant_storage_row = draw_tenant_storage_row(jax.random.fold_in(arg_keys[10], 71), 0)
    slot_tenant_index = draw_slot_tenant_index(jax.random.fold_in(arg_keys[10], 71), 0)
    slot_token_rows = jax.vmap(lambda own: uneven(own, SLOTS_PER_SEQ, TOKEN_ROWS_LOCAL, MOST, 2))(jax.random.split(arg_keys[9], N_SEQ)).reshape((N_SEQ, SLOTS_PER_SEQ)).astype(jnp.int32)
    return dict(attention_output=attention_output, output_gradient=output_gradient, output_weight=output_weight, adapter_down=adapter_down, adapter_up=adapter_up, momentum_down=momentum_down, momentum_up=momentum_up, tenant_storage_row=tenant_storage_row, slot_tenant_index=slot_tenant_index, slot_token_rows=slot_token_rows)


adapter_scale = 2.0
beta_first = 0.9
beta_second = 0.99
soft_floor = 0.25
epsilon = 1e-06

def slot_positions(tenant_storage_row, slot_tenant_index):
    tenant_ids = jnp.arange(tenant_storage_row.shape[0], dtype=jnp.int32)
    match = slot_tenant_index[:, :, None] == tenant_ids[None, None, :]
    return lax.optimization_barrier(jnp.sum(jnp.where(match, tenant_storage_row[None, None, :], 0), axis=2)).astype(jnp.int32)

def row_members(counts, row_count):
    ends = jnp.cumsum(counts)
    starts = ends - counts
    index = jnp.arange(row_count, dtype=jnp.int32)
    return (index[:, None] >= starts[None, :]) & (index[:, None] < ends[None, :])

def lion_step(moment, grad):
    combined = beta_first * moment + (1.0 - beta_first) * grad
    spread = jnp.sqrt(lax.optimization_barrier(jnp.mean(combined * combined, axis=1, keepdims=True)) + epsilon)
    step = combined / (jnp.abs(combined) + soft_floor * spread)
    return (step, beta_second * moment + (1.0 - beta_second) * grad)

def reference(attention_output, output_gradient, output_weight, adapter_down, adapter_up, momentum_down, momentum_up, tenant_storage_row, slot_tenant_index, slot_token_rows):
    slot_location = slot_positions(tenant_storage_row, slot_tenant_index)
    block_in = FEATURES_INPUT // N_TP
    contract_last = (((1,), (1,)), ((), ()))
    contract_leading = (((0,), (0,)), ((), ()))

    def one_device(items):
        inputs, given_gradients, down_tiles_list, up_tiles_list, counts = items
        tenant_mask = row_members(counts, TOKEN_ROWS_LOCAL)[:, :, None]
        flat_down = down_tiles_list.reshape(SLOTS_PER_SEQ * ADAPTER_RANK, FEATURES_INPUT)
        flattened_up = up_tiles_list.reshape(SLOTS_PER_SEQ * ADAPTER_RANK, FEATURES_OUTPUT)
        project = lax.dot_general(inputs, flat_down, contract_last, preferred_element_type=jnp.float32)
        low = lax.optimization_barrier(jnp.sum(jnp.where(tenant_mask, project.reshape(TOKEN_ROWS_LOCAL, SLOTS_PER_SEQ, ADAPTER_RANK), 0.0), axis=1)).astype(jnp.bfloat16)
        backward_pass = lax.dot_general(given_gradients, flattened_up, contract_last, preferred_element_type=jnp.float32)
        lowrank_gradient = (adapter_scale * lax.optimization_barrier(jnp.sum(jnp.where(tenant_mask, backward_pass.reshape(TOKEN_ROWS_LOCAL, SLOTS_PER_SEQ, ADAPTER_RANK), 0.0), axis=1))).astype(jnp.bfloat16)
        spread_lowrank = jnp.where(tenant_mask, low[:, None, :], jnp.zeros((), jnp.bfloat16)).reshape(TOKEN_ROWS_LOCAL, SLOTS_PER_SEQ * ADAPTER_RANK)
        spread_grad = jnp.where(tenant_mask, lowrank_gradient[:, None, :], jnp.zeros((), jnp.bfloat16)).reshape(TOKEN_ROWS_LOCAL, SLOTS_PER_SEQ * ADAPTER_RANK)
        base_output = jnp.zeros((TOKEN_ROWS_LOCAL, FEATURES_OUTPUT), jnp.float32)
        for block in range(N_TP):
            partial_out = jnp.dot(inputs[:, block * block_in:(block + 1) * block_in], output_weight[block * block_in:(block + 1) * block_in], preferred_element_type=jnp.float32)
            rounded = lax.optimization_barrier(partial_out.astype(jnp.bfloat16))
            base_output = base_output + rounded.astype(jnp.float32)
        output_rows = (base_output + adapter_scale * jnp.dot(spread_lowrank, flattened_up, preferred_element_type=jnp.float32)).astype(jnp.bfloat16)
        back_base = lax.dot_general(given_gradients, output_weight, contract_last, preferred_element_type=jnp.float32)
        in_rows = (back_base + jnp.dot(spread_grad, flat_down, preferred_element_type=jnp.float32)).astype(jnp.bfloat16)
        part_down = lax.dot_general(spread_grad, inputs, contract_leading, preferred_element_type=jnp.float32).astype(jnp.bfloat16)
        partial_up = (adapter_scale * lax.dot_general(spread_lowrank, given_gradients, contract_leading, preferred_element_type=jnp.float32)).astype(jnp.bfloat16)
        return (output_rows, in_rows, part_down.reshape(SLOTS_PER_SEQ, ADAPTER_RANK, FEATURES_INPUT), partial_up.reshape(SLOTS_PER_SEQ, ADAPTER_RANK, FEATURES_OUTPUT))
    down_tiles_list = adapter_down[slot_location]
    up_tiles_list = adapter_up[slot_location]
    results = lax.map(one_device, (attention_output.reshape(N_SEQ, TOKEN_ROWS_LOCAL, FEATURES_INPUT), output_gradient.reshape(N_SEQ, TOKEN_ROWS_LOCAL, FEATURES_OUTPUT), down_tiles_list, up_tiles_list, slot_token_rows))
    out_act = results[0].reshape(N_SEQ * TOKEN_ROWS_LOCAL, FEATURES_OUTPUT)
    in_grad = results[1].reshape(N_SEQ * TOKEN_ROWS_LOCAL, FEATURES_INPUT)
    flat_position = slot_location.reshape(-1)
    total_down = jnp.zeros((TENANT_TOTAL, ADAPTER_RANK, FEATURES_INPUT), jnp.float32).at[flat_position].add(results[2].reshape(N_SEQ * SLOTS_PER_SEQ, ADAPTER_RANK, FEATURES_INPUT).astype(jnp.float32))
    total_up = jnp.zeros((TENANT_TOTAL, ADAPTER_RANK, FEATURES_OUTPUT), jnp.float32).at[flat_position].add(results[3].reshape(N_SEQ * SLOTS_PER_SEQ, ADAPTER_RANK, FEATURES_OUTPUT).astype(jnp.float32))
    tokens = jnp.zeros((TENANT_TOTAL,), jnp.int32).at[flat_position].add(slot_token_rows.reshape(-1).astype(jnp.int32))
    denom = jnp.maximum(tokens, 1).astype(jnp.float32)
    step_down, new_moment_down = lion_step(momentum_down, total_down / denom[:, None, None])
    step_up, new_moment_up = lion_step(momentum_up, total_up / denom[:, None, None])
    return (out_act, in_grad, step_down, step_up, new_moment_down, new_moment_up)
```

```python
import functools

import jax
import jax.numpy as jnp
from jax import lax
from jax.experimental import pallas as pl
from jax.experimental.pallas import tpu as pltpu
from jax.sharding import PartitionSpec as P

adapter_scale = 2.0
beta_first = 0.9
beta_second = 0.99
soft_floor = 0.25
epsilon = 1e-06
contract_last = (((1,), (1,)), ((), ()))
contract_leading = (((0,), (0,)), ((), ()))


def slot_positions(tenant_storage_row, slot_tenant_index):
    tenant_ids = jnp.arange(tenant_storage_row.shape[0], dtype=jnp.int32)
    match = slot_tenant_index[:, :, None] == tenant_ids[None, None, :]
    return jnp.sum(jnp.where(match, tenant_storage_row[None, None, :], 0), axis=2)


def pick_kernel(which_ref, in_ref, out_ref):
    out_ref[...] = in_ref[...]


def pick(which, table):
    count = which.shape[0]
    _, rank, width = table.shape
    return pl.pallas_call(
        pick_kernel,
        out_shape=jax.ShapeDtypeStruct((count, rank, width), table.dtype),
        grid_spec=pltpu.PrefetchScalarGridSpec(
            num_scalar_prefetch=1,
            grid=(count,),
            in_specs=[pl.BlockSpec((1, rank, width), lambda j, which_ref: (which_ref[j], 0, 0))],
            out_specs=pl.BlockSpec((1, rank, width), lambda j, which_ref: (j, 0, 0)),
        ),
        cost_estimate=pl.CostEstimate(
            flops=0, transcendentals=0, bytes_accessed=2 * count * rank * width * 2
        ),
        name="pick",
    )(which, table)


def lion_kernel(seq_count, owned, choose_ref, scale_ref, incoming_ref, moment_ref, step_ref, new_ref):
    for k in range(owned):
        total = None
        for i in range(seq_count):
            term = choose_ref[i * owned + k] * incoming_ref[i].astype(jnp.float32)
            total = term if total is None else total + term
        grad = total / scale_ref[k]
        moment = moment_ref[k]
        combined = beta_first * moment + (1.0 - beta_first) * grad
        spread = jnp.sqrt(jnp.mean(combined * combined, axis=0, keepdims=True) + epsilon)
        step_ref[k] = combined / (jnp.abs(combined) + soft_floor * spread)
        new_ref[k] = beta_second * moment + (1.0 - beta_second) * grad


def lion(choose, denom, incoming, moment):
    seq_count, rank, width = incoming.shape
    owned = moment.shape[0]
    tile = min(256, width)
    block = pl.BlockSpec((owned, rank, tile), lambda j: (0, 0, j))
    shape = jax.ShapeDtypeStruct(moment.shape, jnp.float32)
    smem = pl.BlockSpec(memory_space=pltpu.SMEM)
    return pl.pallas_call(
        functools.partial(lion_kernel, seq_count, owned),
        out_shape=(shape, shape),
        grid=(width // tile,),
        in_specs=[smem, smem, pl.BlockSpec((seq_count, rank, tile), lambda j: (0, 0, j)), block],
        out_specs=(block, block),
        cost_estimate=pl.CostEstimate(
            flops=2 * owned * seq_count * rank * width,
            transcendentals=owned * rank * width,
            bytes_accessed=seq_count * rank * width * 2 + 3 * owned * rank * width * 4,
        ),
        compiler_params=pltpu.CompilerParams(vmem_limit_bytes=32 * 1024 * 1024),
        name="lion",
    )(choose, denom, incoming, moment)


def local(
    attention_output,
    output_gradient,
    output_weight,
    adapter_down,
    adapter_up,
    momentum_down,
    momentum_up,
    tenant_storage_row,
    slot_tenant_index,
    slot_token_rows,
):
    device = lax.axis_index("seq")
    seq_count = lax.axis_size("seq")
    tp_count = lax.axis_size("tp")
    row_count = attention_output.shape[0]
    rank = adapter_down.shape[1]
    owned = adapter_down.shape[0]
    width = attention_output.shape[1]
    slot_location = slot_positions(tenant_storage_row, slot_tenant_index)
    owner = slot_location // owned
    within = slot_location % owned
    owned_ids = jnp.arange(owned, dtype=jnp.int32)
    seq_ids = jnp.arange(seq_count, dtype=jnp.int32)
    mine = owner == device
    send_row = jnp.sum(jnp.where(mine, within, 0), axis=1)
    up_out = pick(send_row, adapter_up)
    down_out = pick(send_row, adapter_down)
    up = lax.all_to_all(up_out, "seq", split_axis=0, concat_axis=0, tiled=True)
    up = up.reshape(seq_count * rank, width)
    down = lax.all_to_all(down_out, "seq", split_axis=0, concat_axis=0, tiled=True)
    down = down.reshape(seq_count * rank, width)

    gathered = lax.all_gather(output_gradient, "tp", axis=1, tiled=True)
    base_terms = jnp.dot(attention_output, output_weight, preferred_element_type=jnp.float32)
    base_output = lax.psum_scatter(
        base_terms.astype(jnp.bfloat16), "tp", scatter_dimension=1, tiled=True
    ).astype(jnp.float32)

    my_owner = lax.dynamic_index_in_dim(owner, device, 0, keepdims=False)
    counts = lax.dynamic_index_in_dim(slot_token_rows, device, 0, keepdims=False)
    slot_ids = jnp.arange(counts.shape[0], dtype=jnp.int32)
    starts = jnp.sum(jnp.where(slot_ids[None, :] < slot_ids[:, None], counts[None, :], 0), axis=1)
    hit = my_owner[None, :] == seq_ids[:, None]
    first = jnp.sum(jnp.where(hit, starts[None, :], 0), axis=1)
    last = jnp.sum(jnp.where(hit, (starts + counts)[None, :], 0), axis=1)
    row_ids = jnp.arange(row_count, dtype=jnp.int32)
    mask = (row_ids[None, :] >= first[:, None]) & (row_ids[None, :] < last[:, None])
    mask = mask[:, None, :]

    def project(blocks, rows):
        product = lax.dot_general(blocks, rows, contract_last, preferred_element_type=jnp.float32)
        part = jnp.sum(jnp.where(mask, product.reshape(seq_count, rank, row_count), 0.0), axis=0)
        part = part.astype(jnp.bfloat16)
        total = part.astype(jnp.float32)
        for k in range(1, tp_count):
            order = [(i, (i + k) % tp_count) for i in range(tp_count)]
            total = total + lax.ppermute(part, "tp", order).astype(jnp.float32)
        return total

    def spread(values):
        wide = jnp.where(mask, values[None], jnp.zeros((), jnp.bfloat16))
        return wide.reshape(seq_count * rank, row_count)

    low_grad = (adapter_scale * project(up, output_gradient)).astype(jnp.bfloat16)
    spread_grad = spread(low_grad)
    part_down = jnp.dot(
        spread_grad, attention_output, preferred_element_type=jnp.float32
    ).astype(jnp.bfloat16)
    incoming_down = lax.all_to_all(
        part_down.reshape(seq_count, rank, width), "seq", split_axis=0, concat_axis=0, tiled=True
    )
    low = project(down, attention_output).astype(jnp.bfloat16)
    spread_low = spread(low)
    part_up = (
        adapter_scale * jnp.dot(spread_low, output_gradient, preferred_element_type=jnp.float32)
    ).astype(jnp.bfloat16)
    incoming_up = lax.all_to_all(
        part_up.reshape(seq_count, rank, width), "seq", split_axis=0, concat_axis=0, tiled=True
    )

    back_base = lax.dot_general(
        gathered, output_weight, contract_last, preferred_element_type=jnp.float32
    )
    in_grad = (
        back_base
        + lax.dot_general(spread_grad, down, contract_leading, preferred_element_type=jnp.float32)
    ).astype(jnp.bfloat16)
    out_act = (
        base_output
        + adapter_scale
        * lax.dot_general(spread_low, up, contract_leading, preferred_element_type=jnp.float32)
    ).astype(jnp.bfloat16)

    here = mine[:, :, None] & (within[:, :, None] == owned_ids[None, None, :])
    choose = jnp.sum(here.astype(jnp.float32), axis=1).reshape(seq_count * owned)
    tokens_here = jnp.sum(jnp.where(here, slot_token_rows[:, :, None], 0), axis=(0, 1))
    denom = jnp.maximum(tokens_here, 1).astype(jnp.float32)
    step_down, new_moment_down = lion(choose, denom, incoming_down, momentum_down)
    step_up, new_moment_up = lion(choose, denom, incoming_up, momentum_up)
    return (out_act, in_grad, step_down, step_up, new_moment_down, new_moment_up)


def solution(mesh):
    return jax.shard_map(
        local,
        mesh=mesh,
        in_specs=(
            P("seq", "tp"),
            P("seq", "tp"),
            P("tp", None),
            P("seq", None, "tp"),
            P("seq", None, "tp"),
            P("seq", None, "tp"),
            P("seq", None, "tp"),
            P(),
            P(),
            P(),
        ),
        out_specs=(
            P("seq", "tp"),
            P("seq", "tp"),
            P("seq", None, "tp"),
            P("seq", None, "tp"),
            P("seq", None, "tp"),
            P("seq", None, "tp"),
        ),
        check_vma=False,
    )
```

```python
import functools

import jax
import jax.numpy as jnp
from jax import lax
from jax.experimental import pallas as pl
from jax.experimental.pallas import tpu as pltpu
from jax.sharding import PartitionSpec as P

adapter_scale = 2.0
beta_first = 0.9
beta_second = 0.99
soft_floor = 0.25
epsilon = 1e-06
contract_last = (((1,), (1,)), ((), ()))
contract_leading = (((0,), (0,)), ((), ()))


def slot_positions(tenant_storage_row, slot_tenant_index):
    tenant_ids = jnp.arange(tenant_storage_row.shape[0], dtype=jnp.int32)
    match = slot_tenant_index[:, :, None] == tenant_ids[None, None, :]
    return jnp.sum(jnp.where(match, tenant_storage_row[None, None, :], 0), axis=2)


def pick_kernel(count, which_ref, in_ref, out_ref):
    for j in range(count):
        out_ref[j] = in_ref[which_ref[j]]


def pick(which, table):
    count = which.shape[0]
    _, rank, width = table.shape
    return pl.pallas_call(
        functools.partial(pick_kernel, count),
        out_shape=jax.ShapeDtypeStruct((count, rank, width), table.dtype),
        in_specs=[
            pl.BlockSpec(memory_space=pltpu.SMEM),
            pl.BlockSpec(memory_space=pltpu.VMEM),
        ],
        out_specs=pl.BlockSpec(memory_space=pltpu.VMEM),
        cost_estimate=pl.CostEstimate(
            flops=0, transcendentals=0, bytes_accessed=2 * count * rank * width * 2
        ),
        compiler_params=pltpu.CompilerParams(vmem_limit_bytes=16 * 1024 * 1024),
        name="pick",
    )(which, table)


def lion_kernel(seq_count, owned, choose_ref, scale_ref, incoming_ref, moment_ref, step_ref, new_ref):
    for k in range(owned):
        total = None
        for i in range(seq_count):
            term = choose_ref[i * owned + k] * incoming_ref[i].astype(jnp.float32)
            total = term if total is None else total + term
        grad = total / scale_ref[k]
        moment = moment_ref[k]
        combined = beta_first * moment + (1.0 - beta_first) * grad
        spread = jnp.sqrt(jnp.mean(combined * combined, axis=0, keepdims=True) + epsilon)
        step_ref[k] = combined / (jnp.abs(combined) + soft_floor * spread)
        new_ref[k] = beta_second * moment + (1.0 - beta_second) * grad


def lion(choose, denom, incoming, moment):
    seq_count, rank, width = incoming.shape
    owned = moment.shape[0]
    tile = min(256, width)
    block = pl.BlockSpec((owned, rank, tile), lambda j: (0, 0, j))
    shape = jax.ShapeDtypeStruct(moment.shape, jnp.float32)
    smem = pl.BlockSpec(memory_space=pltpu.SMEM)
    return pl.pallas_call(
        functools.partial(lion_kernel, seq_count, owned),
        out_shape=(shape, shape),
        grid=(width // tile,),
        in_specs=[smem, smem, pl.BlockSpec((seq_count, rank, tile), lambda j: (0, 0, j)), block],
        out_specs=(block, block),
        cost_estimate=pl.CostEstimate(
            flops=2 * owned * seq_count * rank * width,
            transcendentals=owned * rank * width,
            bytes_accessed=seq_count * rank * width * 2 + 3 * owned * rank * width * 4,
        ),
        compiler_params=pltpu.CompilerParams(vmem_limit_bytes=32 * 1024 * 1024),
        name="lion",
    )(choose, denom, incoming, moment)


def local(
    attention_output,
    output_gradient,
    output_weight,
    adapter_down,
    adapter_up,
    momentum_down,
    momentum_up,
    tenant_storage_row,
    slot_tenant_index,
    slot_token_rows,
):
    device = lax.axis_index("seq")
    seq_count = lax.axis_size("seq")
    tp_count = lax.axis_size("tp")
    row_count = attention_output.shape[0]
    rank = adapter_down.shape[1]
    owned = adapter_down.shape[0]
    width = attention_output.shape[1]
    slot_location = slot_positions(tenant_storage_row, slot_tenant_index)
    owner = slot_location // owned
    within = slot_location % owned
    owned_ids = jnp.arange(owned, dtype=jnp.int32)
    seq_ids = jnp.arange(seq_count, dtype=jnp.int32)
    mine = owner == device
    send_row = jnp.sum(jnp.where(mine, within, 0), axis=1)
    up_out = pick(send_row, adapter_up)
    down_out = pick(send_row, adapter_down)
    up = lax.all_to_all(up_out, "seq", split_axis=0, concat_axis=0, tiled=True)
    base_terms = jnp.dot(
        attention_output, output_weight, preferred_element_type=jnp.float32
    ).astype(jnp.bfloat16)
    up, down_out, base_terms = lax.optimization_barrier((up, down_out, base_terms))
    base_output = lax.psum_scatter(
        base_terms, "tp", scatter_dimension=1, tiled=True
    ).astype(jnp.float32)
    up = up.reshape(seq_count * rank, width)
    down = lax.all_to_all(down_out, "seq", split_axis=0, concat_axis=0, tiled=True)
    down = down.reshape(seq_count * rank, width)

    gathered = lax.all_gather(output_gradient, "tp", axis=1, tiled=True)

    my_owner = lax.dynamic_index_in_dim(owner, device, 0, keepdims=False)
    counts = lax.dynamic_index_in_dim(slot_token_rows, device, 0, keepdims=False)
    slot_ids = jnp.arange(counts.shape[0], dtype=jnp.int32)
    starts = jnp.sum(jnp.where(slot_ids[None, :] < slot_ids[:, None], counts[None, :], 0), axis=1)
    hit = my_owner[None, :] == seq_ids[:, None]
    first = jnp.sum(jnp.where(hit, starts[None, :], 0), axis=1)
    last = jnp.sum(jnp.where(hit, (starts + counts)[None, :], 0), axis=1)
    row_ids = jnp.arange(row_count, dtype=jnp.int32)
    mask = (row_ids[None, :] >= first[:, None]) & (row_ids[None, :] < last[:, None])
    mask = mask[:, None, :]

    def project(blocks, rows):
        product = lax.dot_general(blocks, rows, contract_last, preferred_element_type=jnp.float32)
        part = jnp.sum(jnp.where(mask, product.reshape(seq_count, rank, row_count), 0.0), axis=0)
        part = part.astype(jnp.bfloat16)
        total = part.astype(jnp.float32)
        for k in range(1, tp_count):
            order = [(i, (i + k) % tp_count) for i in range(tp_count)]
            total = total + lax.ppermute(part, "tp", order).astype(jnp.float32)
        return total

    def spread(values):
        wide = jnp.where(mask, values[None], jnp.zeros((), jnp.bfloat16))
        return wide.reshape(seq_count * rank, row_count)

    low_grad = (adapter_scale * project(up, output_gradient)).astype(jnp.bfloat16)
    spread_grad = spread(low_grad)
    part_down = jnp.dot(
        spread_grad, attention_output, preferred_element_type=jnp.float32
    ).astype(jnp.bfloat16)
    part_down, gathered, down = lax.optimization_barrier((part_down, gathered, down))
    incoming_down = lax.all_to_all(
        part_down.reshape(seq_count, rank, width), "seq", split_axis=0, concat_axis=0, tiled=True
    )
    low = project(down, attention_output).astype(jnp.bfloat16)
    spread_low = spread(low)
    part_up = (
        adapter_scale * jnp.dot(spread_low, output_gradient, preferred_element_type=jnp.float32)
    ).astype(jnp.bfloat16)
    back_base = lax.dot_general(
        gathered, output_weight, contract_last, preferred_element_type=jnp.float32
    )
    in_grad = (
        back_base
        + lax.dot_general(spread_grad, down, contract_leading, preferred_element_type=jnp.float32)
    ).astype(jnp.bfloat16)
    part_up, incoming_down, in_grad = lax.optimization_barrier((part_up, incoming_down, in_grad))
    incoming_up = lax.all_to_all(
        part_up.reshape(seq_count, rank, width), "seq", split_axis=0, concat_axis=0, tiled=True
    )

    out_act = (
        base_output
        + adapter_scale
        * lax.dot_general(spread_low, up, contract_leading, preferred_element_type=jnp.float32)
    ).astype(jnp.bfloat16)

    here = mine[:, :, None] & (within[:, :, None] == owned_ids[None, None, :])
    choose = jnp.sum(here.astype(jnp.float32), axis=1).reshape(seq_count * owned)
    tokens_here = jnp.sum(jnp.where(here, slot_token_rows[:, :, None], 0), axis=(0, 1))
    denom = jnp.maximum(tokens_here, 1).astype(jnp.float32)
    step_down, new_moment_down = lion(choose, denom, incoming_down, momentum_down)
    step_up, new_moment_up = lion(choose, denom, incoming_up, momentum_up)
    return (out_act, in_grad, step_down, step_up, new_moment_down, new_moment_up)


def solution(mesh):
    return jax.shard_map(
        local,
        mesh=mesh,
        in_specs=(
            P("seq", "tp"),
            P("seq", "tp"),
            P("tp", None),
            P("seq", None, "tp"),
            P("seq", None, "tp"),
            P("seq", None, "tp"),
            P("seq", None, "tp"),
            P(),
            P(),
            P(),
        ),
        out_specs=(
            P("seq", "tp"),
            P("seq", "tp"),
            P("seq", None, "tp"),
            P("seq", None, "tp"),
            P("seq", None, "tp"),
            P("seq", None, "tp"),
        ),
        check_vma=False,
    )
```

```python
import functools

import jax
import jax.numpy as jnp
from jax import lax
from jax.experimental import pallas as pl
from jax.experimental.pallas import tpu as pltpu
from jax.sharding import PartitionSpec as P

adapter_scale = 2.0
beta_first = 0.9
beta_second = 0.99
soft_floor = 0.25
epsilon = 1e-06
contract_last = (((1,), (1,)), ((), ()))
contract_leading = (((0,), (0,)), ((), ()))


def slot_positions(tenant_storage_row, slot_tenant_index):
    tenant_ids = jnp.arange(tenant_storage_row.shape[0], dtype=jnp.int32)
    match = slot_tenant_index[:, :, None] == tenant_ids[None, None, :]
    return jnp.sum(jnp.where(match, tenant_storage_row[None, None, :], 0), axis=2)


def pick_kernel(count, which_ref, in_ref, out_ref):
    for j in range(count):
        out_ref[j] = in_ref[which_ref[j]]


def pick(which, table):
    count = which.shape[0]
    _, rank, width = table.shape
    return pl.pallas_call(
        functools.partial(pick_kernel, count),
        out_shape=jax.ShapeDtypeStruct((count, rank, width), table.dtype),
        in_specs=[
            pl.BlockSpec(memory_space=pltpu.SMEM),
            pl.BlockSpec(memory_space=pltpu.VMEM),
        ],
        out_specs=pl.BlockSpec(memory_space=pltpu.VMEM),
        cost_estimate=pl.CostEstimate(
            flops=0, transcendentals=0, bytes_accessed=2 * count * rank * width * 2
        ),
        compiler_params=pltpu.CompilerParams(vmem_limit_bytes=16 * 1024 * 1024),
        name="pick",
    )(which, table)


def lion_kernel(seq_count, owned, row_ref, used_ref, scale_ref, incoming_ref, moment_ref, step_ref, new_ref, total):
    total[...] = jnp.zeros_like(total)
    for i in range(seq_count):
        k = row_ref[i]
        total[k] = total[k] + used_ref[i] * incoming_ref[i].astype(jnp.float32)
    for k in range(owned):
        grad = total[k] / scale_ref[k]
        moment = moment_ref[k]
        combined = beta_first * moment + (1.0 - beta_first) * grad
        spread = jnp.sqrt(jnp.mean(combined * combined, axis=0, keepdims=True) + epsilon)
        step_ref[k] = combined / (jnp.abs(combined) + soft_floor * spread)
        new_ref[k] = beta_second * moment + (1.0 - beta_second) * grad


def lion(row, used, denom, incoming, moment):
    seq_count, rank, width = incoming.shape
    owned = moment.shape[0]
    tile = min(256, width)
    block = pl.BlockSpec((owned, rank, tile), lambda j: (0, 0, j))
    shape = jax.ShapeDtypeStruct(moment.shape, jnp.float32)
    smem = pl.BlockSpec(memory_space=pltpu.SMEM)
    return pl.pallas_call(
        functools.partial(lion_kernel, seq_count, owned),
        out_shape=(shape, shape),
        grid=(width // tile,),
        in_specs=[smem] * 3
        + [pl.BlockSpec((seq_count, rank, tile), lambda j: (0, 0, j)), block],
        out_specs=(block, block),
        scratch_shapes=[pltpu.VMEM((owned, rank, tile), jnp.float32)],
        cost_estimate=pl.CostEstimate(
            flops=2 * seq_count * rank * width,
            transcendentals=owned * rank * width,
            bytes_accessed=seq_count * rank * width * 2 + 3 * owned * rank * width * 4,
        ),
        compiler_params=pltpu.CompilerParams(vmem_limit_bytes=24 * 1024 * 1024),
        name="lion",
    )(row, used, denom, incoming, moment)


def local(
    attention_output,
    output_gradient,
    output_weight,
    adapter_down,
    adapter_up,
    momentum_down,
    momentum_up,
    tenant_storage_row,
    slot_tenant_index,
    slot_token_rows,
):
    device = lax.axis_index("seq")
    seq_count = lax.axis_size("seq")
    tp_count = lax.axis_size("tp")
    row_count = attention_output.shape[0]
    rank = adapter_down.shape[1]
    owned = adapter_down.shape[0]
    width = attention_output.shape[1]
    slot_location = slot_positions(tenant_storage_row, slot_tenant_index)
    owner = slot_location // owned
    within = slot_location % owned
    owned_ids = jnp.arange(owned, dtype=jnp.int32)
    seq_ids = jnp.arange(seq_count, dtype=jnp.int32)
    mine = owner == device
    send_row = jnp.sum(jnp.where(mine, within, 0), axis=1)
    up_out = pick(send_row, adapter_up)
    down_out = pick(send_row, adapter_down)
    up = lax.all_to_all(up_out, "seq", split_axis=0, concat_axis=0, tiled=True)
    base_terms = jnp.dot(
        attention_output, output_weight, preferred_element_type=jnp.float32
    ).astype(jnp.bfloat16)
    up, down_out, base_terms = lax.optimization_barrier((up, down_out, base_terms))
    base_output = lax.psum_scatter(
        base_terms, "tp", scatter_dimension=1, tiled=True
    ).astype(jnp.float32)
    up = up.reshape(seq_count * rank, width)
    down = lax.all_to_all(down_out, "seq", split_axis=0, concat_axis=0, tiled=True)
    down = down.reshape(seq_count * rank, width)

    gathered = lax.all_gather(output_gradient, "tp", axis=1, tiled=True)

    my_owner = lax.dynamic_index_in_dim(owner, device, 0, keepdims=False)
    counts = lax.dynamic_index_in_dim(slot_token_rows, device, 0, keepdims=False)
    slot_ids = jnp.arange(counts.shape[0], dtype=jnp.int32)
    starts = jnp.sum(jnp.where(slot_ids[None, :] < slot_ids[:, None], counts[None, :], 0), axis=1)
    hit = my_owner[None, :] == seq_ids[:, None]
    first = jnp.sum(jnp.where(hit, starts[None, :], 0), axis=1)
    last = jnp.sum(jnp.where(hit, (starts + counts)[None, :], 0), axis=1)
    row_ids = jnp.arange(row_count, dtype=jnp.int32)
    mask = (row_ids[None, :] >= first[:, None]) & (row_ids[None, :] < last[:, None])
    mask = mask[:, None, :]

    def project(blocks, rows):
        product = lax.dot_general(blocks, rows, contract_last, preferred_element_type=jnp.float32)
        part = jnp.sum(jnp.where(mask, product.reshape(seq_count, rank, row_count), 0.0), axis=0)
        part = part.astype(jnp.bfloat16)
        total = part.astype(jnp.float32)
        for k in range(1, tp_count):
            order = [(i, (i + k) % tp_count) for i in range(tp_count)]
            total = total + lax.ppermute(part, "tp", order).astype(jnp.float32)
        return total

    def spread(values):
        wide = jnp.where(mask, values[None], jnp.zeros((), jnp.bfloat16))
        return wide.reshape(seq_count * rank, row_count)

    low_grad = (adapter_scale * project(up, output_gradient)).astype(jnp.bfloat16)
    spread_grad = spread(low_grad)
    part_down = jnp.dot(
        spread_grad, attention_output, preferred_element_type=jnp.float32
    ).astype(jnp.bfloat16)
    part_down, gathered, down = lax.optimization_barrier((part_down, gathered, down))
    incoming_down = lax.all_to_all(
        part_down.reshape(seq_count, rank, width), "seq", split_axis=0, concat_axis=0, tiled=True
    )
    low = project(down, attention_output).astype(jnp.bfloat16)
    spread_low = spread(low)
    part_up = (
        adapter_scale * jnp.dot(spread_low, output_gradient, preferred_element_type=jnp.float32)
    ).astype(jnp.bfloat16)
    back_base = lax.dot_general(
        gathered, output_weight, contract_last, preferred_element_type=jnp.float32
    )
    in_grad = (
        back_base
        + lax.dot_general(spread_grad, down, contract_leading, preferred_element_type=jnp.float32)
    ).astype(jnp.bfloat16)
    part_up, incoming_down, in_grad = lax.optimization_barrier((part_up, incoming_down, in_grad))
    incoming_up = lax.all_to_all(
        part_up.reshape(seq_count, rank, width), "seq", split_axis=0, concat_axis=0, tiled=True
    )

    out_act = (
        base_output
        + adapter_scale
        * lax.dot_general(spread_low, up, contract_leading, preferred_element_type=jnp.float32)
    ).astype(jnp.bfloat16)

    here = mine[:, :, None] & (within[:, :, None] == owned_ids[None, None, :])
    used = jnp.sum(mine.astype(jnp.float32), axis=1)
    tokens_here = jnp.sum(jnp.where(here, slot_token_rows[:, :, None], 0), axis=(0, 1))
    denom = jnp.maximum(tokens_here, 1).astype(jnp.float32)
    step_down, new_moment_down = lion(send_row, used, denom, incoming_down, momentum_down)
    incoming_up, out_act = lax.optimization_barrier((incoming_up, out_act))
    step_up, new_moment_up = lion(send_row, used, denom, incoming_up, momentum_up)
    return (out_act, in_grad, step_down, step_up, new_moment_down, new_moment_up)


def solution(mesh):
    return jax.shard_map(
        local,
        mesh=mesh,
        in_specs=(
            P("seq", "tp"),
            P("seq", "tp"),
            P("tp", None),
            P("seq", None, "tp"),
            P("seq", None, "tp"),
            P("seq", None, "tp"),
            P("seq", None, "tp"),
            P(),
            P(),
            P(),
        ),
        out_specs=(
            P("seq", "tp"),
            P("seq", "tp"),
            P("seq", None, "tp"),
            P("seq", None, "tp"),
            P("seq", None, "tp"),
            P("seq", None, "tp"),
        ),
        check_vma=False,
    )
```

```python
import functools

import jax
import jax.numpy as jnp
from jax import lax
from jax.experimental import pallas as pl
from jax.experimental.pallas import tpu as pltpu
from jax.sharding import PartitionSpec as P

adapter_scale = 2.0
beta_first = 0.9
beta_second = 0.99
soft_floor = 0.25
epsilon = 1e-06
contract_last = (((1,), (1,)), ((), ()))
contract_leading = (((0,), (0,)), ((), ()))


def slot_positions(tenant_storage_row, slot_tenant_index):
    tenant_ids = jnp.arange(tenant_storage_row.shape[0], dtype=jnp.int32)
    match = slot_tenant_index[:, :, None] == tenant_ids[None, None, :]
    return jnp.sum(jnp.where(match, tenant_storage_row[None, None, :], 0), axis=2)


def pick_kernel(count, which_ref, in_ref, out_ref):
    for j in range(count):
        out_ref[j] = in_ref[which_ref[j]]


def pick(which, table):
    count = which.shape[0]
    _, rank, width = table.shape
    return pl.pallas_call(
        functools.partial(pick_kernel, count),
        out_shape=jax.ShapeDtypeStruct((count, rank, width), table.dtype),
        in_specs=[
            pl.BlockSpec(memory_space=pltpu.SMEM),
            pl.BlockSpec(memory_space=pltpu.VMEM),
        ],
        out_specs=pl.BlockSpec(memory_space=pltpu.VMEM),
        cost_estimate=pl.CostEstimate(
            flops=0, transcendentals=0, bytes_accessed=2 * count * rank * width * 2
        ),
        compiler_params=pltpu.CompilerParams(vmem_limit_bytes=16 * 1024 * 1024),
        name="pick",
    )(which, table)


def lion_kernel(seq_count, owned, row_ref, used_ref, scale_ref, incoming_ref, moment_ref, step_ref, new_ref, total):
    total[...] = jnp.zeros_like(total)
    for i in range(seq_count):
        k = row_ref[i]
        total[k] = total[k] + used_ref[i] * incoming_ref[i].astype(jnp.float32)
    for k in range(owned):
        grad = total[k] / scale_ref[k]
        moment = moment_ref[k]
        combined = beta_first * moment + (1.0 - beta_first) * grad
        spread = jnp.sqrt(jnp.mean(combined * combined, axis=0, keepdims=True) + epsilon)
        step_ref[k] = combined / (jnp.abs(combined) + soft_floor * spread)
        new_ref[k] = beta_second * moment + (1.0 - beta_second) * grad


def lion(row, used, denom, incoming, moment):
    seq_count, rank, width = incoming.shape
    owned = moment.shape[0]
    tile = min(128, width)
    block = pl.BlockSpec((owned, rank, tile), lambda j: (0, 0, j))
    shape = jax.ShapeDtypeStruct(moment.shape, jnp.float32)
    smem = pl.BlockSpec(memory_space=pltpu.SMEM)
    return pl.pallas_call(
        functools.partial(lion_kernel, seq_count, owned),
        out_shape=(shape, shape),
        grid=(width // tile,),
        in_specs=[smem] * 3
        + [pl.BlockSpec((seq_count, rank, tile), lambda j: (0, 0, j)), block],
        out_specs=(block, block),
        scratch_shapes=[pltpu.VMEM((owned, rank, tile), jnp.float32)],
        cost_estimate=pl.CostEstimate(
            flops=2 * seq_count * rank * width,
            transcendentals=owned * rank * width,
            bytes_accessed=seq_count * rank * width * 2 + 3 * owned * rank * width * 4,
        ),
        compiler_params=pltpu.CompilerParams(vmem_limit_bytes=24 * 1024 * 1024),
        name="lion",
    )(row, used, denom, incoming, moment)


def local(
    attention_output,
    output_gradient,
    output_weight,
    adapter_down,
    adapter_up,
    momentum_down,
    momentum_up,
    tenant_storage_row,
    slot_tenant_index,
    slot_token_rows,
):
    device = lax.axis_index("seq")
    seq_count = lax.axis_size("seq")
    tp_count = lax.axis_size("tp")
    row_count = attention_output.shape[0]
    rank = adapter_down.shape[1]
    owned = adapter_down.shape[0]
    width = attention_output.shape[1]
    slot_location = slot_positions(tenant_storage_row, slot_tenant_index)
    owner = slot_location // owned
    within = slot_location % owned
    owned_ids = jnp.arange(owned, dtype=jnp.int32)
    seq_ids = jnp.arange(seq_count, dtype=jnp.int32)
    mine = owner == device
    send_row = jnp.sum(jnp.where(mine, within, 0), axis=1)
    up_out = pick(send_row, adapter_up)
    down_out = pick(send_row, adapter_down)
    up = lax.all_to_all(up_out, "seq", split_axis=0, concat_axis=0, tiled=True)
    base_terms = jnp.dot(
        attention_output, output_weight, preferred_element_type=jnp.float32
    ).astype(jnp.bfloat16)
    up, down_out, base_terms = lax.optimization_barrier((up, down_out, base_terms))
    base_output = lax.psum_scatter(
        base_terms, "tp", scatter_dimension=1, tiled=True
    ).astype(jnp.float32)
    up = up.reshape(seq_count * rank, width)
    down = lax.all_to_all(down_out, "seq", split_axis=0, concat_axis=0, tiled=True)
    down = down.reshape(seq_count * rank, width)

    gathered = lax.all_gather(output_gradient, "tp", axis=1, tiled=True)

    my_owner = lax.dynamic_index_in_dim(owner, device, 0, keepdims=False)
    counts = lax.dynamic_index_in_dim(slot_token_rows, device, 0, keepdims=False)
    slot_ids = jnp.arange(counts.shape[0], dtype=jnp.int32)
    starts = jnp.sum(jnp.where(slot_ids[None, :] < slot_ids[:, None], counts[None, :], 0), axis=1)
    hit = my_owner[None, :] == seq_ids[:, None]
    first = jnp.sum(jnp.where(hit, starts[None, :], 0), axis=1)
    last = jnp.sum(jnp.where(hit, (starts + counts)[None, :], 0), axis=1)
    row_ids = jnp.arange(row_count, dtype=jnp.int32)
    mask = (row_ids[None, :] >= first[:, None]) & (row_ids[None, :] < last[:, None])
    mask = mask[:, None, :]

    def project(blocks, rows, held=None):
        product = lax.dot_general(blocks, rows, contract_last, preferred_element_type=jnp.float32)
        part = jnp.sum(jnp.where(mask, product.reshape(seq_count, rank, row_count), 0.0), axis=0)
        part = part.astype(jnp.bfloat16)
        if held is not None:
            part, held = lax.optimization_barrier((part, held))
        total = part.astype(jnp.float32)
        for k in range(1, tp_count):
            order = [(i, (i + k) % tp_count) for i in range(tp_count)]
            total = total + lax.ppermute(part, "tp", order).astype(jnp.float32)
        return total, held

    def spread(values):
        wide = jnp.where(mask, values[None], jnp.zeros((), jnp.bfloat16))
        return wide.reshape(seq_count * rank, row_count)

    low_grad = (adapter_scale * project(up, output_gradient)[0]).astype(jnp.bfloat16)
    spread_grad = spread(low_grad)
    part_down = jnp.dot(
        spread_grad, attention_output, preferred_element_type=jnp.float32
    ).astype(jnp.bfloat16)
    part_down, down = lax.optimization_barrier((part_down, down))
    incoming_down = lax.all_to_all(
        part_down.reshape(seq_count, rank, width), "seq", split_axis=0, concat_axis=0, tiled=True
    )
    low_total, gathered = project(down, attention_output, gathered)
    low = low_total.astype(jnp.bfloat16)
    spread_low = spread(low)
    part_up = (
        adapter_scale * jnp.dot(spread_low, output_gradient, preferred_element_type=jnp.float32)
    ).astype(jnp.bfloat16)
    back_base = lax.dot_general(
        gathered, output_weight, contract_last, preferred_element_type=jnp.float32
    )
    in_grad = (
        back_base
        + lax.dot_general(spread_grad, down, contract_leading, preferred_element_type=jnp.float32)
    ).astype(jnp.bfloat16)
    part_up, incoming_down, in_grad = lax.optimization_barrier((part_up, incoming_down, in_grad))
    incoming_up = lax.all_to_all(
        part_up.reshape(seq_count, rank, width), "seq", split_axis=0, concat_axis=0, tiled=True
    )

    out_act = (
        base_output
        + adapter_scale
        * lax.dot_general(spread_low, up, contract_leading, preferred_element_type=jnp.float32)
    ).astype(jnp.bfloat16)

    here = mine[:, :, None] & (within[:, :, None] == owned_ids[None, None, :])
    used = jnp.sum(mine.astype(jnp.float32), axis=1)
    tokens_here = jnp.sum(jnp.where(here, slot_token_rows[:, :, None], 0), axis=(0, 1))
    denom = jnp.maximum(tokens_here, 1).astype(jnp.float32)
    step_down, new_moment_down = lion(send_row, used, denom, incoming_down, momentum_down)
    incoming_up, out_act = lax.optimization_barrier((incoming_up, out_act))
    step_up, new_moment_up = lion(send_row, used, denom, incoming_up, momentum_up)
    return (out_act, in_grad, step_down, step_up, new_moment_down, new_moment_up)


def solution(mesh):
    return jax.shard_map(
        local,
        mesh=mesh,
        in_specs=(
            P("seq", "tp"),
            P("seq", "tp"),
            P("tp", None),
            P("seq", None, "tp"),
            P("seq", None, "tp"),
            P("seq", None, "tp"),
            P("seq", None, "tp"),
            P(),
            P(),
            P(),
        ),
        out_specs=(
            P("seq", "tp"),
            P("seq", "tp"),
            P("seq", None, "tp"),
            P("seq", None, "tp"),
            P("seq", None, "tp"),
            P("seq", None, "tp"),
        ),
        check_vma=False,
    )
```
